128 devices in a mesh: row: 16 (over x_lo, z, core), col: 8 (over x_hi, y).
Axes of the slice: x: 4 (x_hi: 2, x_lo: 2; x = x_hi * 2 + x_lo), y: 4, z: 4, core: 2. Of those that a mesh axis runs over, the one named last changes fastest.
Arguments:
- eigvecs: float32 [512, 262144], P(('row', 'col')), may hold values from -6 to 6
- panels: bfloat16 [8, 262144, 128], P('col', 'row'), may hold values from -0.01171875 to 0.01171875
- tfactors: bfloat16 [8, 128, 128], P('col'), as said below
- owners: int32 [4], replicated, may hold values from 0 to 7, as said below
- offsets: int32 [4], replicated, may hold values from 0 to 65408, as said below
Outputs:
- back: float32 [512, 262144], P('col', 'row')
The draws below stay inside these ranges and needn't reach their ends.
Inputs may be any that keep to these rules, and one draw needn't show every extreme that they name: `owners`: distinct grid columns. `offsets`: multiples of 128. `tfactors`: each matrix is upper triangular with its diagonal between 1 and 8.
All inputs are finite; a program needn't handle non-finite values.
Results may differ from the reference program's by a relative error of at most 0.0003.
Values may be sent and summed in bfloat16 or wider, within the bound.
No kernel may reach another device: no remote copies, remote signals or barrier semaphores. Data moves between devices by JAX's collectives and lax.ppermute only.
A program may use at most 128 MiB of HBM per device.

```python
import jax
import jax.numpy as jnp
from jax import lax

N = 262144
NB = 128
K = 512
PANELS = 4
N_COL = 8


def draw_tfactors(key, part):
    key_diag = jax.random.fold_in(key, 5)
    key_above = jax.random.fold_in(key, 7)
    diagonal = jax.random.uniform(key_diag, (N_COL, NB), jnp.float32, 2.0, 6.0)
    above = jax.random.normal(key_above, (N_COL, NB, NB), jnp.float32)
    upper = jnp.triu(above, 1)
    identity = jnp.eye(NB, dtype=jnp.float32)
    return (upper + diagonal[:, :, None] * identity[None, :, :]).astype(jnp.bfloat16)


def draw_owners(key, part):
    order = jax.random.permutation(jax.random.fold_in(key, 11), N_COL)
    return order[:PANELS].astype(jnp.int32)


def draw_offsets(key, part):
    top_block = N // (4 * NB) - 1
    blocks = jax.random.randint(jax.random.fold_in(key, 23), (PANELS,), 0, top_block + 1).astype(jnp.int32)
    order = jax.random.permutation(jax.random.fold_in(key, 29), PANELS).astype(jnp.int32)
    blocks = blocks.at[order[0]].set(jnp.int32(top_block))
    blocks = blocks.at[order[1]].set(jnp.int32(0))
    return (blocks * NB).astype(jnp.int32)


def block_scale(key, extent, shards, low, high):
    loudness = 1.0
    for axis_at, parts in shards:
        draws = jax.random.uniform(jax.random.fold_in(jax.random.fold_in(key, 6), axis_at), (parts,), jnp.float32, low / len(shards), high / len(shards))
        loudness = loudness * jnp.repeat(jnp.exp(draws), extent[axis_at] // parts).reshape((-1,) + (1,) * (len(extent) - 1 - axis_at))
    return loudness


def centred(stream_key, shape, width, most, split=(), held_as=jnp.bfloat16):
    gain = block_scale(stream_key, shape, split, -0.22, 0.18) if split else 1.0
    drawn = jax.random.normal(stream_key, shape, jnp.float32) * width * gain
    return jnp.minimum(jnp.maximum(drawn, -most), most).astype(held_as)


def setup_inputs(seed: int = 0) -> dict:
    key_of = jax.random.split(jax.random.key(seed), 6)
    return {
        "eigvecs": centred(key_of[0], (K, N), 1.0, 6.0, ((0, 128),), jnp.float32),
        "panels": centred(key_of[1], (N_COL, N, NB), N ** -0.5, 0.01171875, ((0, 8), (1, 16))),
        "tfactors": draw_tfactors(jax.random.fold_in(key_of[5], 71), 0),
        "owners": draw_owners(jax.random.fold_in(key_of[5], 71), 0),
        "offsets": draw_offsets(jax.random.fold_in(key_of[5], 71), 0),
    }


def reference(eigvecs, panels, tfactors, owners, offsets):
    highest = lax.Precision.HIGHEST
    row_ids = jnp.arange(N, dtype=jnp.int32)[:, None]
    col_ids = jnp.arange(NB, dtype=jnp.int32)[None, :]
    field = eigvecs
    for panel in reversed(range(PANELS)):
        owner_col = owners[panel].astype(jnp.int32)
        stored = lax.dynamic_index_in_dim(panels, owner_col, 0, keepdims=False).astype(jnp.float32)
        triangle = lax.dynamic_index_in_dim(tfactors, owner_col, 0, keepdims=False).astype(jnp.float32)
        below = row_ids - col_ids - offsets[panel].astype(jnp.int32)
        unit = jnp.where(below == 0, jnp.float32(1.0), jnp.float32(0.0))
        reflector = jnp.where(below > 0, stored, unit)
        projection = jnp.dot(field, reflector, precision=highest, preferred_element_type=jnp.float32)
        coeffs = jnp.dot(projection, triangle.T, precision=highest, preferred_element_type=jnp.float32)
        field = field - jnp.dot(coeffs, reflector.T, precision=highest, preferred_element_type=jnp.float32)
    return field
```

```python
import math

import jax
import jax.numpy as jnp
from jax import lax
from jax.experimental import pallas as pl
from jax.experimental.pallas import tpu as pltpu
from jax.sharding import PartitionSpec as P

PANELS = 4
NB = 128
K = 512
DEVS = 128
COLS = 8
OWN = 4
SUB = 2048
STEP = 512
STEPS = SUB // STEP
TILES = SUB // 128
WIDE = K // COLS
PACK = 24
PAIRS = [(q, p) for q in range(PANELS) for p in range(q)]
ALL = ("row", "col")
HIGHEST = lax.Precision.HIGHEST

MU = 2.0**18 / 6.0
LOG_SCALE = 32767.0 / math.log1p(2.0**18)


def encode_log(x):
    level = jnp.log(1.0 + MU * jnp.abs(x)) * LOG_SCALE + 0.5
    level = jnp.minimum(level, 32767.0).astype(jnp.int32)
    return jnp.where(x < 0.0, -level, level).astype(jnp.int16)


def decode_log(code):
    level = code.astype(jnp.int32).astype(jnp.float32)
    size = (jnp.exp(jnp.abs(level) * (1.0 / LOG_SCALE)) - 1.0) * (1.0 / MU)
    return jnp.where(level < 0.0, -size, size)


def dot32(a, b, dims=((1,), (0,)), precision=None):
    return lax.dot_general(
        a, b, (dims, ((), ())), precision=precision, preferred_element_type=jnp.float32
    )


def split(x):
    high = x.astype(jnp.bfloat16)
    return high, (x - high.astype(jnp.float32)).astype(jnp.bfloat16)


def encode_kernel(e_ref, out_ref):
    for d in range(out_ref.shape[0]):
        x = e_ref[:, d * SUB : (d + 1) * SUB]
        tall = jnp.concatenate([x[:, t * 128 : (t + 1) * 128] for t in range(TILES)], axis=0)
        out_ref[d] = encode_log(tall)


def encode(eigvecs):
    group = 8
    return pl.pallas_call(
        encode_kernel,
        out_shape=jax.ShapeDtypeStruct((DEVS, OWN * TILES, 128), jnp.int16),
        grid=(DEVS // group,),
        in_specs=[pl.BlockSpec((OWN, group * SUB), lambda g: (0, g))],
        out_specs=pl.BlockSpec((group, OWN * TILES, 128), lambda g: (g, 0, 0)),
        name="encode",
    )(eigvecs)


def decode_kernel(code_ref, high_ref, low_ref):
    def body(g, carry):
        x = decode_log(code_ref[pl.ds(g * 4, 4)])
        rows = pl.ds(pl.multiple_of(g * 16, 16), 16)
        for t in range(TILES):
            tile = jnp.concatenate([x[i, t * OWN : (t + 1) * OWN] for i in range(4)], axis=0)
            high, low = split(tile)
            high_ref[rows, t * 128 : (t + 1) * 128] = high
            low_ref[rows, t * 128 : (t + 1) * 128] = low
        return carry

    lax.fori_loop(0, code_ref.shape[0] // 4, body, 0)


def decode(codes):
    group = 32
    out = jax.ShapeDtypeStruct((K, SUB), jnp.bfloat16)
    return pl.pallas_call(
        decode_kernel,
        out_shape=(out, out),
        grid=(DEVS // group,),
        in_specs=[pl.BlockSpec((group, OWN * TILES, 128), lambda g: (g, 0, 0))],
        out_specs=(pl.BlockSpec((group * OWN, SUB), lambda g: (g, 0)),) * 2,
        name="decode",
    )(codes)


def project_kernel(s_ref, high_ref, low_ref, v0, v1, v2, v3, pack_ref, refl_ref, proj, gram):
    step = pl.program_id(0)

    @pl.when(step == 0)
    def _():
        proj[...] = jnp.zeros_like(proj)
        gram[...] = jnp.zeros_like(gram)

    row_ids = s_ref[8] + step * STEP + lax.broadcasted_iota(jnp.int32, (STEP, NB), 0)
    base = row_ids - lax.broadcasted_iota(jnp.int32, (STEP, NB), 1)
    for p, ref in enumerate((v0, v1, v2, v3)):
        below = base - s_ref[4 + p]
        unit = jnp.where(below == 0, jnp.float32(1.0), jnp.float32(0.0))
        block = jnp.where(below > 0, ref[0].astype(jnp.float32), unit)
        refl_ref[:, p * NB : (p + 1) * NB] = block.astype(jnp.bfloat16)
    v = refl_ref[...]
    proj[...] += dot32(high_ref[...], v) + dot32(low_ref[...], v)
    gram[...] += dot32(v, v, ((0,), (0,)))

    @pl.when(step == STEPS - 1)
    def _():
        for p in range(PANELS):
            pack_ref[p * 32 : (p + 1) * 32, 0:16, :] = proj[:, p * NB : (p + 1) * NB].reshape(32, 16, NB)
        for b, (q, p) in enumerate(PAIRS):
            block = gram[q * NB : (q + 1) * NB, p * NB : (p + 1) * NB]
            pack_ref[b * 16 : (b + 1) * 16, 16:24, :] = block.reshape(16, 8, NB)
        for b in range(len(PAIRS), 8):
            pack_ref[b * 16 : (b + 1) * 16, 16:24, :] = jnp.zeros((16, 8, NB), jnp.float32)


def slot_spec(p, rows, index):
    return pl.BlockSpec((1, rows, NB), lambda k, s: (s[p], index(k), 0))


def project(scalars, high, low, slots):
    return pl.pallas_call(
        project_kernel,
        out_shape=(
            jax.ShapeDtypeStruct((DEVS, PACK, NB), jnp.float32),
            jax.ShapeDtypeStruct((SUB, PANELS * NB), jnp.bfloat16),
        ),
        grid_spec=pltpu.PrefetchScalarGridSpec(
            num_scalar_prefetch=1,
            grid=(STEPS,),
            in_specs=[pl.BlockSpec((K, STEP), lambda k, s: (0, k))] * 2
            + [slot_spec(p, STEP, lambda k: k) for p in range(PANELS)],
            out_specs=(
                pl.BlockSpec((DEVS, PACK, NB), lambda k, s: (0, 0, 0)),
                pl.BlockSpec((STEP, PANELS * NB), lambda k, s: (k, 0)),
            ),
            scratch_shapes=[
                pltpu.VMEM((K, PANELS * NB), jnp.float32),
                pltpu.VMEM((PANELS * NB, PANELS * NB), jnp.float32),
            ],
        ),
        name="project",
    )(scalars, high, low, slots, slots, slots, slots)


def total_kernel(in_ref, out_ref):
    total = jnp.sum(in_ref[...], axis=0)
    out_ref[...] = jnp.broadcast_to(total[None], out_ref.shape)


def total(parts):
    return pl.pallas_call(
        total_kernel,
        out_shape=jax.ShapeDtypeStruct(parts.shape, parts.dtype),
        name="total",
    )(parts)


def update_kernel(s_ref, sums_ref, t0, t1, t2, t3, high_ref, low_ref, refl_ref, out_ref, c_high, c_low, coef):
    step = pl.program_id(0)

    @pl.when(step == 0)
    def _():
        triangles = (t0, t1, t2, t3)
        gram = {}
        for b, pair in enumerate(PAIRS):
            gram[pair] = sums_ref[b * 16 : (b + 1) * 16, 16:24, :].reshape(NB, NB)
        for p in reversed(range(PANELS)):
            rest = sums_ref[p * 32 : (p + 1) * 32, 0:16, :].reshape(K, NB)
            for q in range(p + 1, PANELS):
                rest -= dot32(coef[:, q * NB : (q + 1) * NB], gram[(q, p)], precision=HIGHEST)
            triangle = triangles[p][0].astype(jnp.float32)
            coef[:, p * NB : (p + 1) * NB] = dot32(rest, triangle, ((1,), (1,)), HIGHEST)
        high, low = split(coef[...])
        c_high[...] = high
        c_low[...] = low

    v = refl_ref[...]
    change = dot32(c_high[...], v, ((1,), (1,))) + dot32(c_low[...], v, ((1,), (1,)))
    back = high_ref[...].astype(jnp.float32) + (low_ref[...].astype(jnp.float32) - change)
    for c in range(COLS):
        block = back[c * WIDE : (c + 1) * WIDE]
        most = jnp.max(jnp.abs(block), axis=(0, 1), keepdims=True)
        power = jnp.ceil(jnp.log(jnp.maximum(most, 1e-30)) * (1.0 / math.log(2.0)) + 0.001)
        scale = jnp.exp(power * -math.log(2.0))
        level = (jnp.sqrt(jnp.abs(block) * scale) * 32767.0 + 0.5).astype(jnp.int32)
        code = jnp.where(block < 0.0, -level, level).astype(jnp.int16)
        for t in range(STEP // 128):
            at = pl.multiple_of((step * (STEP // 128) + t) * WIDE, WIDE)
            out_ref[c, pl.ds(at, WIDE), :] = code[:, t * 128 : (t + 1) * 128]
        at = pl.multiple_of(TILES * WIDE + step * 8, 8)
        out_ref[c, pl.ds(at, 8), :] = jnp.broadcast_to(power, (8, 128)).astype(jnp.int32).astype(jnp.int16)


def update(scalars, sums, slots, high, low, refl):
    rows = TILES * WIDE + 8 * STEPS
    return pl.pallas_call(
        update_kernel,
        out_shape=jax.ShapeDtypeStruct((COLS, rows, 128), jnp.int16),
        grid_spec=pltpu.PrefetchScalarGridSpec(
            num_scalar_prefetch=1,
            grid=(STEPS,),
            in_specs=[pl.BlockSpec((DEVS, PACK, NB), lambda k, s: (0, 0, 0))]
            + [slot_spec(p, NB, lambda k: SUB // NB) for p in range(PANELS)]
            + [pl.BlockSpec((K, STEP), lambda k, s: (0, k))] * 2
            + [pl.BlockSpec((STEP, PANELS * NB), lambda k, s: (k, 0))],
            out_specs=pl.BlockSpec((COLS, rows, 128), lambda k, s: (0, 0, 0)),
            scratch_shapes=[
                pltpu.VMEM((K, PANELS * NB), jnp.bfloat16),
                pltpu.VMEM((K, PANELS * NB), jnp.bfloat16),
                pltpu.VMEM((K, PANELS * NB), jnp.float32),
            ],
        ),
        name="update",
    )(scalars, sums, slots, slots, slots, slots, high, low, refl)


def finish_kernel(code_ref, out_ref):
    for k in range(STEPS):
        at = TILES * WIDE + 8 * k
        power = code_ref[0, at : at + 8, :].astype(jnp.int32).astype(jnp.float32)
        unit = jnp.exp(power * math.log(2.0)) * (1.0 / 32767.0**2)
        unit = jnp.concatenate([unit] * (WIDE // 8), axis=0)
        for t in range(k * (STEP // 128), (k + 1) * (STEP // 128)):
            level = code_ref[0, t * WIDE : (t + 1) * WIDE, :].astype(jnp.int32).astype(jnp.float32)
            out_ref[:, t * 128 : (t + 1) * 128] = level * jnp.abs(level) * unit


def finish(codes):
    rows = codes.shape[1]
    return pl.pallas_call(
        finish_kernel,
        out_shape=jax.ShapeDtypeStruct((WIDE, COLS * SUB), jnp.float32),
        grid=(COLS,),
        in_specs=[pl.BlockSpec((1, rows, 128), lambda g: (g, 0, 0))],
        out_specs=pl.BlockSpec((WIDE, SUB), lambda g: (0, g)),
        name="finish",
    )(codes)


def exchange(x, axis):
    return lax.all_to_all(x, axis, split_axis=0, concat_axis=0, tiled=True)


def local(eigvecs, panels, tfactors, owners, offsets):
    device = lax.axis_index("row") * COLS + lax.axis_index("col")
    scalars = jnp.concatenate([owners, offsets, jnp.full((1,), device * SUB, jnp.int32)])
    codes = exchange(encode(eigvecs), ALL)
    triangles = jnp.broadcast_to(tfactors, (COLS, NB, NB))
    stored = jnp.concatenate([panels.reshape(COLS, SUB, NB), triangles], axis=1)
    slots = exchange(stored, "col")
    high, low = decode(codes)
    pack, refl = project(scalars, high, low, slots)
    sums = exchange(total(exchange(pack, ALL)), ALL)
    out = update(scalars, sums, slots, high, low, refl)
    return finish(exchange(out, "col"))


def solution(mesh):
    in_specs = (P(ALL, None), P("col", "row", None), P("col", None, None), P(), P())
    out_specs = P("col", "row")
    return jax.shard_map(local, mesh=mesh, in_specs=in_specs, out_specs=out_specs, check_vma=False)
```

```python
import math

import jax
import jax.numpy as jnp
from jax import lax
from jax.experimental import pallas as pl
from jax.experimental.pallas import tpu as pltpu
from jax.sharding import PartitionSpec as P

PANELS = 4
NB = 128
K = 512
DEVS = 128
COLS = 8
OWN = 4
SUB = 2048
STEP = 512
STEPS = SUB // STEP
TILES = SUB // 128
WIDE = K // COLS
PACK = 24
PAIRS = [(q, p) for q in range(PANELS) for p in range(q)]
ALL = ("row", "col")

MU = 2.0**18 / 6.0
LOG_SCALE = 32767.0 / math.log1p(2.0**18)
LN2 = math.log(2.0)
T_STEPS = 258.0
T_ZERO = 50.0 * T_STEPS
ROWS = OWN * TILES + 8
GROUP = 32


def signed(level, like):
    return jnp.where(like < 0.0, -level, level)


def to_float(code):
    return code.astype(jnp.int32).astype(jnp.float32)


def encode_log(x):
    level = jnp.log(1.0 + MU * jnp.abs(x)) * LOG_SCALE + 0.5
    return signed(jnp.minimum(level, 32767.0).astype(jnp.int32), x).astype(jnp.int16)


def decode_log(code):
    level = to_float(code)
    return signed((jnp.exp(jnp.abs(level) * (1.0 / LOG_SCALE)) - 1.0) * (1.0 / MU), level)


def encode_triangle(x):
    level = jnp.log(jnp.maximum(jnp.abs(x), 1e-30)) * (T_STEPS / LN2) + (T_ZERO + 0.5)
    level = jnp.clip(level, 0.0, 32767.0).astype(jnp.int32)
    return signed(level, x).astype(jnp.int16)


def decode_triangle(code):
    level = to_float(code)
    size = jnp.exp((jnp.abs(level) - T_ZERO) * (LN2 / T_STEPS))
    return jnp.where(level == 0.0, 0.0, signed(size, level)).astype(jnp.bfloat16)


def power_of(most):
    return jnp.ceil(jnp.log(jnp.maximum(most, 1e-30)) * (8.0 / LN2) + 0.01)


def levels(x, power):
    size = jnp.sqrt(jnp.abs(x) * jnp.exp(power * (-LN2 / 8.0))) * 32767.0 + 0.5
    return signed(size.astype(jnp.int32), x)


def unit_of(power):
    return jnp.exp(power * (LN2 / 8.0)) * (1.0 / 32767.0**2)


def dot32(a, b, dims=((1,), (0,))):
    return lax.dot_general(a, b, (dims, ((), ())), preferred_element_type=jnp.float32)


def split(x):
    high = x.astype(jnp.bfloat16)
    return high, (x - high.astype(jnp.float32)).astype(jnp.bfloat16)


def encode_kernel(e_ref, t_ref, out_ref):
    triangle = encode_triangle(t_ref[...].astype(jnp.float32))
    for d in range(out_ref.shape[0]):
        x = e_ref[:, d * SUB : (d + 1) * SUB]
        tall = jnp.concatenate([x[:, t * 128 : (t + 1) * 128] for t in range(TILES)], axis=0)
        out_ref[d, 0 : OWN * TILES, :] = encode_log(tall)
        out_ref[d, OWN * TILES : ROWS, :] = triangle


def encode(eigvecs, triangle):
    group = 8
    return pl.pallas_call(
        encode_kernel,
        out_shape=jax.ShapeDtypeStruct((DEVS, ROWS, 128), jnp.int16),
        grid=(DEVS // group,),
        in_specs=[
            pl.BlockSpec((OWN, group * SUB), lambda g: (0, g)),
            pl.BlockSpec((8, NB), lambda g: (0, 0)),
        ],
        out_specs=pl.BlockSpec((group, ROWS, 128), lambda g: (g, 0, 0)),
        name="encode",
    )(eigvecs, triangle)


def gram_kernel(s_ref, v0, v1, v2, v3, gram_ref, refl_ref, gram):
    step = pl.program_id(0)

    @pl.when(step == 0)
    def _():
        gram[...] = jnp.zeros_like(gram)

    row_ids = s_ref[8] + step * STEP + lax.broadcasted_iota(jnp.int32, (STEP, NB), 0)
    base = row_ids - lax.broadcasted_iota(jnp.int32, (STEP, NB), 1)
    for p, ref in enumerate((v0, v1, v2, v3)):
        below = base - s_ref[4 + p]
        unit = jnp.where(below == 0, jnp.float32(1.0), jnp.float32(0.0))
        block = jnp.where(below > 0, ref[0].astype(jnp.float32), unit)
        refl_ref[:, p * NB : (p + 1) * NB] = block.astype(jnp.bfloat16)
    v = refl_ref[...]
    gram[...] += dot32(v, v, ((0,), (0,)))

    @pl.when(step == STEPS - 1)
    def _():
        blocks = [gram[q * NB : (q + 1) * NB, p * NB : (p + 1) * NB] for q, p in PAIRS]
        most = jnp.zeros((1, 1), jnp.float32)
        for block in blocks:
            most = jnp.maximum(most, jnp.max(jnp.abs(block), axis=(0, 1), keepdims=True))
        power = power_of(most)
        rows = [levels(block, power).astype(jnp.float32) for block in blocks]
        rows += [jnp.zeros((NB, NB), jnp.float32), jnp.broadcast_to(power, (NB, NB))]
        gram_ref[...] = jnp.swapaxes(jnp.stack(rows), 0, 1)


def gram_of(scalars, slots):
    slot = [pl.BlockSpec((1, STEP, NB), lambda k, s, p=p: (s[p], k, 0)) for p in range(PANELS)]
    return pl.pallas_call(
        gram_kernel,
        out_shape=(
            jax.ShapeDtypeStruct((DEVS, 8, NB), jnp.float32),
            jax.ShapeDtypeStruct((SUB, PANELS * NB), jnp.bfloat16),
        ),
        grid_spec=pltpu.PrefetchScalarGridSpec(
            num_scalar_prefetch=1,
            grid=(STEPS,),
            in_specs=slot,
            out_specs=(
                pl.BlockSpec((DEVS, 8, NB), lambda k, s: (0, 0, 0)),
                pl.BlockSpec((STEP, PANELS * NB), lambda k, s: (k, 0)),
            ),
            scratch_shapes=[pltpu.VMEM((PANELS * NB, PANELS * NB), jnp.float32)],
        ),
        name="gram",
    )(scalars, slots, slots, slots, slots)


def project_kernel(code_ref, refl_ref, gram_ref, pack_ref, high_ref, low_ref):
    group = pl.program_id(0)

    def body(g, carry):
        x = decode_log(code_ref[pl.ds(g * 4, 4), 0 : OWN * TILES, :])
        rows = pl.ds(pl.multiple_of(g * 16, 16), 16)
        for t in range(TILES):
            tile = jnp.concatenate([x[i, t * OWN : (t + 1) * OWN] for i in range(4)], axis=0)
            high, low = split(tile)
            high_ref[rows, t * 128 : (t + 1) * 128] = high
            low_ref[rows, t * 128 : (t + 1) * 128] = low
        return carry

    lax.fori_loop(0, GROUP // 4, body, 0)
    v = refl_ref[...]
    part = dot32(high_ref[...], v) + dot32(low_ref[...], v)
    each = GROUP * OWN // 16
    row = lax.broadcasted_iota(jnp.int32, (each, 8, NB), 1)
    for p in range(PANELS):
        block = part[:, p * NB : (p + 1) * NB].reshape(each, 16, NB)
        power = power_of(jnp.max(jnp.abs(block), axis=(1, 2), keepdims=True))
        where = pl.ds(p * (K // 16) + group * each, each)
        pack_ref[where, 0:16, :] = levels(block, power).astype(jnp.int16)
        tail = jnp.where(row == 6, power, gram_ref[where])
        pack_ref[where, 16:24, :] = tail.astype(jnp.int32).astype(jnp.int16)


def project(codes, refl, gram):
    wide = jax.ShapeDtypeStruct((K, SUB), jnp.bfloat16)
    return pl.pallas_call(
        project_kernel,
        out_shape=(jax.ShapeDtypeStruct((DEVS, PACK, NB), jnp.int16), wide, wide),
        grid=(DEVS // GROUP,),
        in_specs=[
            pl.BlockSpec((GROUP, ROWS, 128), lambda g: (g, 0, 0)),
            pl.BlockSpec((SUB, PANELS * NB), lambda g: (0, 0)),
            pl.BlockSpec((DEVS, 8, NB), lambda g: (0, 0, 0)),
        ],
        out_specs=(pl.BlockSpec((DEVS, PACK, NB), lambda g: (0, 0, 0)),)
        + (pl.BlockSpec((GROUP * OWN, SUB), lambda g: (g, 0)),) * 2,
        name="project",
    )(codes, refl, gram)


def total_kernel(in_ref, out_ref):
    level = to_float(in_ref[...])
    value = level * jnp.abs(level)
    proj = jnp.sum(value[:, 0:16] * unit_of(level[:, 22:23]), axis=0)
    gram = jnp.sum(value[:, 16:24] * unit_of(level[:, 23:24]), axis=0)
    row = lax.broadcasted_iota(jnp.int32, (8, NB), 0)
    gram = jnp.where(row < 6, gram, 0.0)
    proj_power = power_of(jnp.max(jnp.abs(proj), axis=(0, 1), keepdims=True))
    gram_power = power_of(jnp.max(jnp.abs(gram), axis=(0, 1), keepdims=True))
    tail = jnp.where(row == 6, proj_power, jnp.where(row == 7, gram_power, levels(gram, gram_power).astype(jnp.float32)))
    code = jnp.concatenate([levels(proj, proj_power), tail.astype(jnp.int32)], axis=0)
    out_ref[...] = jnp.broadcast_to(code[None], out_ref.shape).astype(jnp.int16)


def total(parts):
    return pl.pallas_call(
        total_kernel,
        out_shape=jax.ShapeDtypeStruct(parts.shape, parts.dtype),
        name="total",
    )(parts)


def update_kernel(s_ref, sums_ref, t0, t1, t2, t3, high_ref, low_ref, refl_ref, out_ref, c_high, c_low):
    step = pl.program_id(0)

    @pl.when(step == 0)
    def _():
        level = to_float(sums_ref[...])
        value = level * jnp.abs(level)
        proj = value[:, 0:16] * unit_of(level[:, 22:23])
        blocks = jnp.swapaxes(value[:, 16:24] * unit_of(level[:, 23:24]), 0, 1)
        gram = {pair: split(blocks[b]) for b, pair in enumerate(PAIRS)}
        found = {}
        for p in reversed(range(PANELS)):
            rest = proj[p * 32 : (p + 1) * 32].reshape(K, NB)
            for q in range(p + 1, PANELS):
                (c1, c2), (g1, g2) = found[q], gram[(q, p)]
                rest -= dot32(c1, g1) + (dot32(c1, g2) + dot32(c2, g1))
            triangle = decode_triangle((t0, t1, t2, t3)[p][...]).reshape(NB, NB)
            r1, r2 = split(rest)
            dims = ((1,), (1,))
            found[p] = split(dot32(r1, triangle, dims) + dot32(r2, triangle, dims))
            c_high[:, p * NB : (p + 1) * NB] = found[p][0]
            c_low[:, p * NB : (p + 1) * NB] = found[p][1]

    v = refl_ref[...]
    change = dot32(c_high[...], v, ((1,), (1,))) + dot32(c_low[...], v, ((1,), (1,)))
    back = high_ref[...].astype(jnp.float32) + (low_ref[...].astype(jnp.float32) - change)
    for c in range(COLS):
        block = back[c * WIDE : (c + 1) * WIDE]
        power = power_of(jnp.max(jnp.abs(block), axis=(0, 1), keepdims=True))
        code = levels(block, power).astype(jnp.int16)
        for t in range(STEP // 128):
            at = pl.multiple_of((step * (STEP // 128) + t) * WIDE, WIDE)
            out_ref[c, pl.ds(at, WIDE), :] = code[:, t * 128 : (t + 1) * 128]
        at = pl.multiple_of(TILES * WIDE + step * 8, 8)
        out_ref[c, pl.ds(at, 8), :] = jnp.broadcast_to(power, (8, 128)).astype(jnp.int32).astype(jnp.int16)


def update(scalars, sums, codes, high, low, refl):
    rows = TILES * WIDE + 8 * STEPS
    codes = codes.reshape(DEVS // COLS, COLS, ROWS, 128)
    triangle = [
        pl.BlockSpec((DEVS // COLS, pl.Squeezed(), 8, NB), lambda k, s, p=p: (0, s[p], OWN * TILES // 8, 0))
        for p in range(PANELS)
    ]
    return pl.pallas_call(
        update_kernel,
        out_shape=jax.ShapeDtypeStruct((COLS, rows, 128), jnp.int16),
        grid_spec=pltpu.PrefetchScalarGridSpec(
            num_scalar_prefetch=1,
            grid=(STEPS,),
            in_specs=[pl.BlockSpec((DEVS, PACK, NB), lambda k, s: (0, 0, 0))]
            + triangle
            + [pl.BlockSpec((K, STEP), lambda k, s: (0, k))] * 2
            + [pl.BlockSpec((STEP, PANELS * NB), lambda k, s: (k, 0))],
            out_specs=pl.BlockSpec((COLS, rows, 128), lambda k, s: (0, 0, 0)),
            scratch_shapes=[pltpu.VMEM((K, PANELS * NB), jnp.bfloat16)] * 2,
        ),
        name="update",
    )(scalars, sums, codes, codes, codes, codes, high, low, refl)


def finish_kernel(code_ref, out_ref):
    for k in range(STEPS):
        at = TILES * WIDE + 8 * k
        unit = unit_of(to_float(code_ref[0, at : at + 8, :]))
        unit = jnp.concatenate([unit] * (WIDE // 8), axis=0)
        for t in range(k * (STEP // 128), (k + 1) * (STEP // 128)):
            level = to_float(code_ref[0, t * WIDE : (t + 1) * WIDE, :])
            out_ref[:, t * 128 : (t + 1) * 128] = level * jnp.abs(level) * unit


def finish(codes):
    rows = codes.shape[1]
    return pl.pallas_call(
        finish_kernel,
        out_shape=jax.ShapeDtypeStruct((WIDE, COLS * SUB), jnp.float32),
        grid=(COLS,),
        in_specs=[pl.BlockSpec((1, rows, 128), lambda g: (g, 0, 0))],
        out_specs=pl.BlockSpec((WIDE, SUB), lambda g: (0, g)),
        name="finish",
    )(codes)


def exchange(x, axis):
    return lax.all_to_all(x, axis, split_axis=0, concat_axis=0, tiled=True)


def local(eigvecs, panels, tfactors, owners, offsets):
    row, col = lax.axis_index("row"), lax.axis_index("col")
    first = (row * COLS + col) * SUB
    scalars = jnp.concatenate([owners, offsets, jnp.full((1,), first, jnp.int32)])
    slots = exchange(panels.reshape(COLS, SUB, NB), "col")
    triangle = lax.dynamic_slice_in_dim(tfactors[0], row * 8, 8, 0)
    sent, slots = lax.optimization_barrier((encode(eigvecs, triangle), slots))
    codes = exchange(sent, ALL)
    gram, refl = gram_of(scalars, slots)
    pack, high, low = project(codes, refl, gram)
    sums = exchange(total(exchange(pack, ALL)), ALL)
    out = update(scalars, sums, codes, high, low, refl)
    return finish(exchange(out, "col"))


def solution(mesh):
    in_specs = (P(ALL, None), P("col", "row", None), P("col", None, None), P(), P())
    out_specs = P("col", "row")
    return jax.shard_map(local, mesh=mesh, in_specs=in_specs, out_specs=out_specs, check_vma=False)
```

```python
import math

import jax
import jax.numpy as jnp
from jax import lax
from jax.experimental import pallas as pl
from jax.experimental.pallas import tpu as pltpu
from jax.sharding import PartitionSpec as P

PANELS = 4
NB = 128
K = 512
DEVS = 128
COLS = 8
OWN = 4
SUB = 2048
STEP = 512
STEPS = SUB // STEP
TILES = SUB // 128
WIDE = K // COLS
PACK = 24
PAIRS = [(q, p) for q in range(PANELS) for p in range(q)]
ALL = ("row", "col")
ROOM = 24 << 20

ASINH_TOP = 12.5
KNEE = 6.0 / math.sinh(ASINH_TOP)
ASINH_SCALE = 32767.0 / ASINH_TOP
LN2 = math.log(2.0)
T_STEPS = 258.0
T_ZERO = 50.0 * T_STEPS
ROWS = OWN * TILES + 8


def signed(level, like):
    return jnp.where(like < 0.0, -level, level)


def to_float(code):
    return code.astype(jnp.int32).astype(jnp.float32)


def encode_value(x):
    y = jnp.abs(x) * (1.0 / KNEE)
    level = jnp.log(y + jnp.sqrt(y * y + 1.0)) * ASINH_SCALE + 0.5
    return signed(jnp.minimum(level, 32767.0).astype(jnp.int32), x).astype(jnp.int16)


def decode_value(code):
    angle = to_float(code) * (1.0 / ASINH_SCALE)
    return (jnp.exp(angle) - jnp.exp(-angle)) * (0.5 * KNEE)


def encode_triangle(x):
    level = jnp.log(jnp.maximum(jnp.abs(x), 1e-30)) * (T_STEPS / LN2) + (T_ZERO + 0.5)
    level = jnp.clip(level, 0.0, 32767.0).astype(jnp.int32)
    return signed(level, x).astype(jnp.int16)


def decode_triangle(code):
    level = to_float(code)
    size = jnp.exp((jnp.abs(level) - T_ZERO) * (LN2 / T_STEPS))
    return jnp.where(level == 0.0, 0.0, signed(size, level)).astype(jnp.bfloat16)


def power_of(most):
    return jnp.ceil(jnp.log(jnp.maximum(most, 1e-30)) * (8.0 / LN2) + 0.01)


def levels(x, power):
    size = jnp.sqrt(jnp.abs(x) * jnp.exp(power * (-LN2 / 8.0))) * 32767.0 + 0.5
    return signed(size.astype(jnp.int32), x)


def unit_of(power):
    return jnp.exp(power * (LN2 / 8.0)) * (1.0 / 32767.0**2)


def dot32(a, b, dims=((1,), (0,))):
    return lax.dot_general(a, b, (dims, ((), ())), preferred_element_type=jnp.float32)


def split(x):
    high = x.astype(jnp.bfloat16)
    return high, (x - high.astype(jnp.float32)).astype(jnp.bfloat16)


def encode_kernel(e_ref, t_ref, out_ref):
    triangle = encode_triangle(t_ref[...].astype(jnp.float32))
    for d in range(out_ref.shape[0]):
        x = e_ref[:, d * SUB : (d + 1) * SUB]
        tall = jnp.concatenate([x[:, t * 128 : (t + 1) * 128] for t in range(TILES)], axis=0)
        out_ref[d, 0 : OWN * TILES, :] = encode_value(tall)
        out_ref[d, OWN * TILES : ROWS, :] = triangle


def encode(eigvecs, triangle):
    group = 8
    return pl.pallas_call(
        encode_kernel,
        out_shape=jax.ShapeDtypeStruct((DEVS, ROWS, 128), jnp.int16),
        grid=(DEVS // group,),
        in_specs=[
            pl.BlockSpec((OWN, group * SUB), lambda g: (0, g)),
            pl.BlockSpec((8, NB), lambda g: (0, 0)),
        ],
        out_specs=pl.BlockSpec((group, ROWS, 128), lambda g: (g, 0, 0)),
        compiler_params=pltpu.CompilerParams(vmem_limit_bytes=ROOM),
        name="encode",
    )(eigvecs, triangle)


def gram_kernel(s_ref, slot_ref, gram_ref, refl_ref):
    gram = jnp.zeros((PANELS * NB, PANELS * NB), jnp.float32)
    for step in range(STEPS):
        row_ids = s_ref[8] + step * STEP + lax.broadcasted_iota(jnp.int32, (STEP, NB), 0)
        base = row_ids - lax.broadcasted_iota(jnp.int32, (STEP, NB), 1)
        rows = slice(step * STEP, (step + 1) * STEP)
        for p in range(PANELS):
            below = base - s_ref[4 + p]
            unit = jnp.where(below == 0, jnp.float32(1.0), jnp.float32(0.0))
            block = jnp.where(below > 0, slot_ref[s_ref[p], rows, :].astype(jnp.float32), unit)
            refl_ref[rows, p * NB : (p + 1) * NB] = block.astype(jnp.bfloat16)
        v = refl_ref[rows, :]
        gram += dot32(v, v, ((0,), (0,)))
    blocks = [gram[q * NB : (q + 1) * NB, p * NB : (p + 1) * NB] for q, p in PAIRS]
    most = jnp.zeros((1, 1), jnp.float32)
    for block in blocks:
        most = jnp.maximum(most, jnp.max(jnp.abs(block), axis=(0, 1), keepdims=True))
    power = power_of(most)
    rows = [levels(block, power).astype(jnp.float32) for block in blocks]
    rows += [jnp.zeros((NB, NB), jnp.float32), jnp.broadcast_to(power, (NB, NB))]
    gram_ref[...] = jnp.swapaxes(jnp.stack(rows), 0, 1)


def call(kernel, outs, ins, name, scalars=None, scratch=()):
    spec = pl.BlockSpec(memory_space=pltpu.VMEM)
    kept = [pltpu.with_memory_space_constraint(x, pltpu.VMEM) for x in ins]
    head = [] if scalars is None else [scalars]
    return pl.pallas_call(
        kernel,
        out_shape=tuple(pltpu.VMEM(*out) for out in outs),
        in_specs=[pl.BlockSpec(memory_space=pltpu.SMEM)] * len(head) + [spec] * len(kept),
        out_specs=(spec,) * len(outs),
        scratch_shapes=list(scratch),
        compiler_params=pltpu.CompilerParams(vmem_limit_bytes=ROOM),
        name=name,
    )(*head, *kept)


def gram_of(scalars, slots):
    outs = (((DEVS, 8, NB), jnp.float32), ((SUB, PANELS * NB), jnp.bfloat16))
    return call(gram_kernel, outs, (slots,), "gram", scalars)


def project_kernel(code_ref, refl_ref, gram_ref, pack_ref, high_ref, low_ref):
    upper = lax.broadcasted_iota(jnp.int32, (DEVS // 2, 8, 128), 1) < OWN
    for t in range(0, TILES, 2):
        x = decode_value(code_ref[:, t * OWN : (t + 2) * OWN, :]).reshape(DEVS // 2, 2, 8, 128)
        even, odd = x[:, 0], x[:, 1]
        first = jnp.where(upper, even, pltpu.roll(odd, OWN, 1))
        second = jnp.where(upper, pltpu.roll(even, OWN, 1), odd)
        for k, tile in ((t, first), (t + 1, second)):
            high, low = split(tile.reshape(K, 128))
            high_ref[:, k * 128 : (k + 1) * 128] = high
            low_ref[:, k * 128 : (k + 1) * 128] = low
    v = refl_ref[...]
    part = dot32(high_ref[...], v) + dot32(low_ref[...], v)
    each = K // 16
    row = lax.broadcasted_iota(jnp.int32, (each, 8, NB), 1)
    for p in range(PANELS):
        block = part[:, p * NB : (p + 1) * NB].reshape(each, 16, NB)
        power = power_of(jnp.max(jnp.abs(block), axis=(1, 2), keepdims=True))
        where = slice(p * each, (p + 1) * each)
        pack_ref[where, 0:16, :] = levels(block, power).astype(jnp.int16)
        tail = jnp.where(row == 6, power, gram_ref[where])
        pack_ref[where, 16:24, :] = tail.astype(jnp.int32).astype(jnp.int16)


def project(codes, refl, gram):
    outs = (((DEVS, PACK, NB), jnp.int16),) + (((K, SUB), jnp.bfloat16),) * 2
    return call(project_kernel, outs, (codes, refl, gram), "project")


def total_kernel(in_ref, out_ref):
    level = to_float(in_ref[...])
    value = level * jnp.abs(level)
    proj = jnp.sum(value[:, 0:16] * unit_of(level[:, 22:23]), axis=0)
    gram = jnp.sum(value[:, 16:24] * unit_of(level[:, 23:24]), axis=0)
    row = lax.broadcasted_iota(jnp.int32, (8, NB), 0)
    gram = jnp.where(row < 6, gram, 0.0)
    proj_power = power_of(jnp.max(jnp.abs(proj), axis=(0, 1), keepdims=True))
    gram_power = power_of(jnp.max(jnp.abs(gram), axis=(0, 1), keepdims=True))
    tail = jnp.where(row == 6, proj_power, jnp.where(row == 7, gram_power, levels(gram, gram_power).astype(jnp.float32)))
    code = jnp.concatenate([levels(proj, proj_power), tail.astype(jnp.int32)], axis=0)
    out_ref[...] = jnp.broadcast_to(code[None], out_ref.shape).astype(jnp.int16)


def total(parts):
    return call(total_kernel, ((parts.shape, parts.dtype),), (parts,), "total")[0]


def update_kernel(s_ref, sums_ref, code_ref, high_ref, low_ref, refl_ref, out_ref, c_high, c_low):
    level = to_float(sums_ref[...])
    value = level * jnp.abs(level)
    proj = value[:, 0:16] * unit_of(level[:, 22:23])
    blocks = jnp.swapaxes(value[:, 16:24] * unit_of(level[:, 23:24]), 0, 1)
    gram = {pair: split(blocks[b]) for b, pair in enumerate(PAIRS)}
    found = {}
    for p in reversed(range(PANELS)):
        rest = proj[p * 32 : (p + 1) * 32].reshape(K, NB)
        for q in range(p + 1, PANELS):
            (c1, c2), (g1, g2) = found[q], gram[(q, p)]
            rest -= dot32(c1, g1) + (dot32(c1, g2) + dot32(c2, g1))
        kept = [code_ref[r * COLS + s_ref[p], OWN * TILES : ROWS, :] for r in range(DEVS // COLS)]
        triangle = decode_triangle(jnp.concatenate(kept, axis=0))
        r1, r2 = split(rest)
        dims = ((1,), (1,))
        found[p] = split(dot32(r1, triangle, dims) + dot32(r2, triangle, dims))
        c_high[:, p * NB : (p + 1) * NB] = found[p][0]
        c_low[:, p * NB : (p + 1) * NB] = found[p][1]
    for step in range(STEPS):
        cols = slice(step * STEP, (step + 1) * STEP)
        v = refl_ref[cols, :]
        change = dot32(c_high[...], v, ((1,), (1,))) + dot32(c_low[...], v, ((1,), (1,)))
        back = high_ref[:, cols].astype(jnp.float32) + (low_ref[:, cols].astype(jnp.float32) - change)
        for c in range(COLS):
            block = back[c * WIDE : (c + 1) * WIDE]
            power = power_of(jnp.max(jnp.abs(block), axis=(0, 1), keepdims=True))
            code = levels(block, power).astype(jnp.int16)
            for t in range(STEP // 128):
                at = (step * (STEP // 128) + t) * WIDE
                out_ref[c, at : at + WIDE, :] = code[:, t * 128 : (t + 1) * 128]
            at = TILES * WIDE + step * 8
            out_ref[c, at : at + 8, :] = jnp.broadcast_to(power, (8, 128)).astype(jnp.int32).astype(jnp.int16)


def update(scalars, sums, codes, high, low, refl):
    outs = (((COLS, TILES * WIDE + 8 * STEPS, 128), jnp.int16),)
    scratch = [pltpu.VMEM((K, PANELS * NB), jnp.bfloat16)] * 2
    return call(update_kernel, outs, (sums, codes, high, low, refl), "update", scalars, scratch)[0]


def finish_kernel(code_ref, out_ref, rows, sems):
    copies = []
    for c in range(COLS):
        for k in range(STEPS):
            at = TILES * WIDE + 8 * k
            unit = unit_of(to_float(code_ref[c, at : at + 8, :]))
            unit = jnp.concatenate([unit] * (WIDE // 8), axis=0)
            for t in range(k * (STEP // 128), (k + 1) * (STEP // 128)):
                level = to_float(code_ref[c, t * WIDE : (t + 1) * WIDE, :])
                rows[:, c * SUB + t * 128 : c * SUB + (t + 1) * 128] = level * jnp.abs(level) * unit
        part = (slice(None), pl.ds(c * SUB, SUB))
        copies.append(pltpu.make_async_copy(rows.at[part], out_ref.at[part], sems.at[c]))
        copies[-1].start()
    for copy in copies:
        copy.wait()


def finish(codes):
    return pl.pallas_call(
        finish_kernel,
        out_shape=jax.ShapeDtypeStruct((WIDE, COLS * SUB), jnp.float32),
        in_specs=[pl.BlockSpec(memory_space=pltpu.VMEM)],
        out_specs=pl.BlockSpec(memory_space=pl.ANY),
        scratch_shapes=[pltpu.VMEM((WIDE, COLS * SUB), jnp.float32), pltpu.SemaphoreType.DMA((COLS,))],
        compiler_params=pltpu.CompilerParams(vmem_limit_bytes=ROOM),
        name="finish",
    )(pltpu.with_memory_space_constraint(codes, pltpu.VMEM))


def exchange(x, axis):
    return lax.all_to_all(x, axis, split_axis=0, concat_axis=0, tiled=True)


def local(eigvecs, panels, tfactors, owners, offsets):
    row, col = lax.axis_index("row"), lax.axis_index("col")
    first = (row * COLS + col) * SUB
    scalars = jnp.concatenate([owners, offsets, jnp.full((1,), first, jnp.int32)])
    slots = exchange(panels.reshape(COLS, SUB, NB), "col")
    triangle = lax.dynamic_slice_in_dim(tfactors[0], row * 8, 8, 0)
    sent, slots = lax.optimization_barrier((encode(eigvecs, triangle), slots))
    codes = exchange(sent, ALL)
    gram, refl = gram_of(scalars, slots)
    pack, high, low = project(codes, refl, gram)
    sums = exchange(total(exchange(pack, ALL)), ALL)
    out = update(scalars, sums, codes, high, low, refl)
    return finish(exchange(out, "col"))


def solution(mesh):
    in_specs = (P(ALL, None), P("col", "row", None), P("col", None, None), P(), P())
    out_specs = P("col", "row")
    return jax.shard_map(local, mesh=mesh, in_specs=in_specs, out_specs=out_specs, check_vma=False)
```

```python
import math

import jax
import jax.numpy as jnp
from jax import lax
from jax.experimental import pallas as pl
from jax.experimental.pallas import tpu as pltpu
from jax.sharding import PartitionSpec as P


PANELS = 4
NB = 128
K = 512
DEVS = 128
COLS = 8
OWN = 4
SUB = 2048
STEP = 512
STEPS = SUB // STEP
TILES = SUB // 128
WIDE = K // COLS
PACK = 24
PAIRS = [(q, p) for q in range(PANELS) for p in range(q)]
ALL = ("row", "col")
ROOM = 24 << 20

ASINH_TOP = 12.5
KNEE = 6.0 / math.sinh(ASINH_TOP)
ASINH_SCALE = 32767.0 / ASINH_TOP
LN2 = math.log(2.0)
PLANES = 4
HALVES = 2
PLANE = DEVS // PLANES


def signed(level, like):
    return jnp.where(like < 0.0, -level, level)


def to_float(code):
    return code.astype(jnp.int32).astype(jnp.float32)


def encode_value(x):
    y = jnp.abs(x) * (1.0 / KNEE)
    level = jnp.log(y + jnp.sqrt(y * y + 1.0)) * ASINH_SCALE + 0.5
    return signed(jnp.minimum(level, 32767.0).astype(jnp.int32), x).astype(jnp.int16)


def decode_value(code):
    angle = to_float(code) * (1.0 / ASINH_SCALE)
    return (jnp.exp(angle) - jnp.exp(-angle)) * (0.5 * KNEE)


def power_of(most):
    return jnp.ceil(jnp.log(jnp.maximum(most, 1e-30)) * (8.0 / LN2) + 0.01)


def levels(x, power):
    scaled = x * (jnp.exp(power * (-LN2 / 8.0)) * 32767.0**2)
    root = scaled * lax.rsqrt(jnp.abs(scaled) + 1e-30)
    return jnp.round(root).astype(jnp.int32)


def unit_of(power):
    return jnp.exp(power * (LN2 / 8.0)) * (1.0 / 32767.0**2)


def dot32(a, b, dims=((1,), (0,))):
    return lax.dot_general(a, b, (dims, ((), ())), preferred_element_type=jnp.float32)


def split(x):
    high = x.astype(jnp.bfloat16)
    return high, (x - high.astype(jnp.float32)).astype(jnp.bfloat16)


def encode_kernel(z_ref, e_ref, out_ref):
    for d in range(COLS):
        x = e_ref[:, d * SUB : (d + 1) * SUB]
        tall = jnp.concatenate([x[:, t * 128 : (t + 1) * 128] for t in range(TILES)], axis=0)
        out_ref[0, d] = encode_value(tall)


def encode(eigvecs, z):
    size = COLS * SUB

    def source(k, a, b, z_ref):
        return 0, (a * PLANES + lax.rem(z_ref[0] + k, PLANES)) * HALVES + b

    return pl.pallas_call(
        encode_kernel,
        out_shape=jax.ShapeDtypeStruct((PLANES, PLANE, OWN * TILES, 128), jnp.int16),
        grid_spec=pltpu.PrefetchScalarGridSpec(
            num_scalar_prefetch=1,
            grid=(PLANES, HALVES, HALVES),
            in_specs=[pl.BlockSpec((OWN, size), source)],
            out_specs=pl.BlockSpec((1, COLS, OWN * TILES, 128), lambda k, a, b, z_ref: (k, a * HALVES + b, 0, 0)),
        ),
        compiler_params=pltpu.CompilerParams(vmem_limit_bytes=ROOM),
        name="encode",
    )(z, eigvecs)


def gram_kernel(s_ref, slot_ref, *refs):
    arrived, (gram_ref, out_ref, t_ref, refl_ref, held, sems) = refs[:COLS], refs[COLS:]
    for k in range(COLS):
        held[k] = arrived[k][0]
    for p in range(PANELS):
        t_ref[p] = held[s_ref[9 + p]]
    copies = []
    gram = jnp.zeros((PANELS * NB, PANELS * NB), jnp.float32)
    for step in range(STEPS):
        row_ids = s_ref[8] + step * STEP + lax.broadcasted_iota(jnp.int32, (STEP, NB), 0)
        base = row_ids - lax.broadcasted_iota(jnp.int32, (STEP, NB), 1)
        rows = slice(step * STEP, (step + 1) * STEP)
        for p in range(PANELS):
            below = base - s_ref[4 + p]
            unit = jnp.where(below == 0, jnp.float32(1.0), jnp.float32(0.0))
            block = jnp.where(below > 0, slot_ref[s_ref[p], rows, :].astype(jnp.float32), unit)
            refl_ref[rows, p * NB : (p + 1) * NB] = block.astype(jnp.bfloat16)
        v = refl_ref[rows, :]
        part = pl.ds(step * STEP, STEP)
        copies.append(pltpu.make_async_copy(refl_ref.at[part], out_ref.at[part], sems.at[step]))
        copies[-1].start()
        gram += dot32(v, v, ((0,), (0,)))
    blocks = [gram[q * NB : (q + 1) * NB, p * NB : (p + 1) * NB] for q, p in PAIRS]
    most = jnp.zeros((1, 1), jnp.float32)
    for block in blocks:
        most = jnp.maximum(most, jnp.max(jnp.abs(block), axis=(0, 1), keepdims=True))
    power = power_of(most)
    rows = [levels(block, power).astype(jnp.float32) for block in blocks]
    rows += [jnp.zeros((NB, NB), jnp.float32), jnp.broadcast_to(power, (NB, NB))]
    gram_ref[...] = jnp.swapaxes(jnp.stack(rows), 0, 1)
    for copy in copies:
        copy.wait()


def call(kernel, outs, ins, scalars=None, scratch=(), hbm_in=(), hbm_out=()):
    spec, raw = pl.BlockSpec(memory_space=pltpu.VMEM), pl.BlockSpec(memory_space=pltpu.HBM)
    kept = [pltpu.with_memory_space_constraint(x, pltpu.HBM if i in hbm_in else pltpu.VMEM) for i, x in enumerate(ins)]
    head = [] if scalars is None else [scalars]
    return pl.pallas_call(
        kernel,
        out_shape=tuple(pltpu.HBM(*out) if i in hbm_out else pltpu.VMEM(*out) for i, out in enumerate(outs)),
        in_specs=[pl.BlockSpec(memory_space=pltpu.SMEM)] * len(head) + [raw if i in hbm_in else spec for i in range(len(ins))],
        out_specs=tuple(raw if i in hbm_out else spec for i in range(len(outs))),
        scratch_shapes=list(scratch),
        compiler_params=pltpu.CompilerParams(vmem_limit_bytes=ROOM),
    )(*head, *kept)


def gram_of(scalars, slots, triangles):
    outs = (
        ((DEVS, 8, NB), jnp.float32),
        ((SUB, PANELS * NB), jnp.bfloat16),
        ((PANELS, NB, NB), jnp.bfloat16),
    )
    scratch = [
        pltpu.VMEM((SUB, PANELS * NB), jnp.bfloat16),
        pltpu.VMEM((COLS, NB, NB), jnp.bfloat16),
        pltpu.SemaphoreType.DMA((STEPS,)),
    ]
    return call(gram_kernel, outs, (slots, *triangles), scalars, scratch, hbm_out=(1,))


def project_kernel(s_ref, code_ref, refl_hbm, gram_ref, pack_ref, high_ref, low_ref, refl_ref, sem):
    fetch = pltpu.make_async_copy(refl_hbm, refl_ref, sem.at[0])
    fetch.start()
    upper = lax.broadcasted_iota(jnp.int32, (COLS // 2, 8, 128), 1) < OWN
    for r in range(DEVS // COLS):
        a, source, b = r // (PLANES * HALVES), r // HALVES % PLANES, r % HALVES
        turn = lax.rem(s_ref[13] + (PLANES - source), PLANES)
        rows = slice(r * COLS * OWN, (r + 1) * COLS * OWN)
        for t in range(0, TILES, 2):
            code = code_ref[(a * HALVES + b) * COLS : (a * HALVES + b + 1) * COLS, turn, t * OWN : (t + 2) * OWN, :]
            x = decode_value(code).reshape(COLS // 2, 2, 8, 128)
            even, odd = x[:, 0], x[:, 1]
            first = jnp.where(upper, even, pltpu.roll(odd, OWN, 1))
            second = jnp.where(upper, pltpu.roll(even, OWN, 1), odd)
            for k, tile in ((t, first), (t + 1, second)):
                high, low = split(tile.reshape(COLS * OWN, 128))
                high_ref[rows, k * 128 : (k + 1) * 128] = high
                low_ref[rows, k * 128 : (k + 1) * 128] = low
    fetch.wait()
    v = refl_ref[...]
    part = dot32(high_ref[...], v) + dot32(low_ref[...], v)
    each = K // 16
    row = lax.broadcasted_iota(jnp.int32, (each, 8, NB), 1)
    for p in range(PANELS):
        block = part[:, p * NB : (p + 1) * NB].reshape(each, 16, NB)
        power = power_of(jnp.max(jnp.abs(block), axis=(1, 2), keepdims=True))
        where = slice(p * each, (p + 1) * each)
        pack_ref[where, 0:16, :] = levels(block, power).astype(jnp.int16)
        tail = jnp.where(row == 6, power, gram_ref[where])
        pack_ref[where, 16:24, :] = tail.astype(jnp.int32).astype(jnp.int16)


def project(scalars, codes, refl, gram):
    outs = (((DEVS, PACK, NB), jnp.int16),) + (((K, SUB), jnp.bfloat16),) * 2
    scratch = [pltpu.VMEM((SUB, PANELS * NB), jnp.bfloat16), pltpu.SemaphoreType.DMA((1,))]
    return call(project_kernel, outs, (codes, refl, gram), scalars, scratch, hbm_in=(1,))


def total_kernel(in_ref, out_ref):
    level = to_float(in_ref[...])
    value = level * jnp.abs(level)
    proj = jnp.sum(value[:, 0:16] * unit_of(level[:, 22:23]), axis=0)
    gram = jnp.sum(value[:, 16:24] * unit_of(level[:, 23:24]), axis=0)
    row = lax.broadcasted_iota(jnp.int32, (8, NB), 0)
    gram = jnp.where(row < 6, gram, 0.0)
    proj_power = power_of(jnp.max(jnp.abs(proj), axis=(0, 1), keepdims=True))
    gram_power = power_of(jnp.max(jnp.abs(gram), axis=(0, 1), keepdims=True))
    tail = jnp.where(row == 6, proj_power, jnp.where(row == 7, gram_power, levels(gram, gram_power).astype(jnp.float32)))
    code = jnp.concatenate([levels(proj, proj_power), tail.astype(jnp.int32)], axis=0)
    out_ref[...] = jnp.broadcast_to(code[None], out_ref.shape).astype(jnp.int16)


def total(parts):
    return call(total_kernel, ((parts.shape, parts.dtype),), (parts,))[0]


def update_kernel(sums_ref, t_ref, high_ref, low_ref, refl_ref, out_ref, c_high, c_low):
    level = to_float(sums_ref[...])
    value = level * jnp.abs(level)
    proj = value[:, 0:16] * unit_of(level[:, 22:23])
    blocks = jnp.swapaxes(value[:, 16:24] * unit_of(level[:, 23:24]), 0, 1)
    gram = {pair: split(blocks[b]) for b, pair in enumerate(PAIRS)}
    found = {}
    for p in reversed(range(PANELS)):
        rest = proj[p * 32 : (p + 1) * 32].reshape(K, NB)
        for q in range(p + 1, PANELS):
            (c1, c2), (g1, g2) = found[q], gram[(q, p)]
            rest -= dot32(c1, g1) + (dot32(c1, g2) + dot32(c2, g1))
        triangle = t_ref[p]
        r1, r2 = split(rest)
        dims = ((1,), (1,))
        found[p] = split(dot32(r1, triangle, dims) + dot32(r2, triangle, dims))
        c_high[:, p * NB : (p + 1) * NB] = found[p][0]
        c_low[:, p * NB : (p + 1) * NB] = found[p][1]
    for step in range(STEPS):
        cols = slice(step * STEP, (step + 1) * STEP)
        v = refl_ref[cols, :]
        change = dot32(c_high[...], v, ((1,), (1,))) + dot32(c_low[...], v, ((1,), (1,)))
        back = high_ref[:, cols].astype(jnp.float32) + (low_ref[:, cols].astype(jnp.float32) - change)
        for c in range(COLS):
            block = back[c * WIDE : (c + 1) * WIDE]
            power = power_of(jnp.max(jnp.abs(block), axis=(0, 1), keepdims=True))
            code = levels(block, power).astype(jnp.int16)
            for t in range(STEP // 128):
                at = (step * (STEP // 128) + t) * WIDE
                out_ref[c, at : at + WIDE, :] = code[:, t * 128 : (t + 1) * 128]
            at = TILES * WIDE + step * 8
            out_ref[c, at : at + 8, :] = jnp.broadcast_to(power, (8, 128)).astype(jnp.int32).astype(jnp.int16)


def update(sums, triangles, high, low, refl):
    outs = (((COLS, TILES * WIDE + 8 * STEPS, 128), jnp.int16),)
    scratch = [pltpu.VMEM((K, PANELS * NB), jnp.bfloat16)] * 2
    return call(update_kernel, outs, (sums, triangles, high, low, refl), None, scratch)[0]


def finish_kernel(code_ref, out_ref, rows, sems):
    copies = []
    for c in range(COLS):
        for k in range(STEPS):
            at = TILES * WIDE + 8 * k
            unit = unit_of(to_float(code_ref[c, at : at + 8, :]))
            unit = jnp.concatenate([unit] * (WIDE // 8), axis=0)
            for t in range(k * (STEP // 128), (k + 1) * (STEP // 128)):
                level = to_float(code_ref[c, t * WIDE : (t + 1) * WIDE, :])
                rows[:, c * SUB + t * 128 : c * SUB + (t + 1) * 128] = level * jnp.abs(level) * unit
        part = (slice(None), pl.ds(c * SUB, SUB))
        copies.append(pltpu.make_async_copy(rows.at[part], out_ref.at[part], sems.at[c]))
        copies[-1].start()
    for copy in copies:
        copy.wait()


def finish(codes):
    return pl.pallas_call(
        finish_kernel,
        out_shape=jax.ShapeDtypeStruct((WIDE, COLS * SUB), jnp.float32),
        in_specs=[pl.BlockSpec(memory_space=pltpu.VMEM)],
        out_specs=pl.BlockSpec(memory_space=pl.ANY),
        scratch_shapes=[pltpu.VMEM((WIDE, COLS * SUB), jnp.float32), pltpu.SemaphoreType.DMA((COLS,))],
        compiler_params=pltpu.CompilerParams(vmem_limit_bytes=ROOM),
        name="finish",
    )(pltpu.with_memory_space_constraint(codes, pltpu.VMEM))


def exchange(x, axis):
    return lax.all_to_all(x, axis, split_axis=0, concat_axis=0, tiled=True)


def spread(x):
    blocks = [x]
    for k in range(1, COLS):
        blocks.append(lax.ppermute(x, "col", [(c, c ^ k) for c in range(COLS)]))
    return blocks


def along_z(sent):
    planes = [sent[0]]
    for k in range(1, PLANES):
        pairs = []
        for r in range(DEVS // COLS):
            z = r // HALVES % PLANES
            pairs.append((r, r + ((z + k) % PLANES - z) * HALVES))
        planes.append(lax.ppermute(sent[k], "row", pairs))
    packed = jnp.concatenate(planes, axis=1)
    return packed.reshape(PLANE, PLANES, OWN * TILES, 128)


def within_plane(x):
    groups = []
    for z in range(PLANES):
        rows = [r for r in range(DEVS // COLS) if r // HALVES % PLANES == z]
        groups.append([r * COLS + c for r in rows for c in range(COLS)])
    return lax.all_to_all(x, ALL, split_axis=0, concat_axis=0, tiled=True, axis_index_groups=groups)


def local(eigvecs, panels, tfactors, owners, offsets):
    row, col = lax.axis_index("row"), lax.axis_index("col")
    z = row // HALVES % PLANES
    own = jnp.stack([(row * COLS + col) * SUB])
    scalars = jnp.concatenate([owners, offsets, own, owners ^ col, jnp.stack([z])])
    slots = exchange(panels.reshape(COLS, SUB, NB), "col")
    triangles = spread(tfactors)
    planes = encode(eigvecs, jnp.stack([z]))
    sent, slots = lax.optimization_barrier((along_z(planes), slots))
    codes = within_plane(sent)
    gram, refl, triangles = gram_of(scalars, slots, triangles)
    pack, high, low = project(scalars, codes, refl, gram)
    sums = exchange(total(exchange(pack, ALL)), ALL)
    out = update(sums, triangles, high, low, refl)
    return finish(exchange(out, "col"))


def solution(mesh):
    in_specs = (P(ALL, None), P("col", "row", None), P("col", None, None), P(), P())
    out_specs = P("col", "row")
    return jax.shard_map(local, mesh=mesh, in_specs=in_specs, out_specs=out_specs, check_vma=False)
```

```python
import math

import jax
import jax.numpy as jnp
from jax import lax
from jax.experimental import pallas as pl
from jax.experimental.pallas import tpu as pltpu
from jax.sharding import PartitionSpec as P


PANELS = 4
NB = 128
K = 512
DEVS = 128
COLS = 8
OWN = 4
SUB = 2048
STEP = 512
STEPS = SUB // STEP
TILES = SUB // 128
WIDE = K // COLS
PACK = 24
PAIRS = [(q, p) for q in range(PANELS) for p in range(q)]
ALL = ("row", "col")
ROOM = 24 << 20

ASINH_TOP = 12.5
KNEE = 6.0 / math.sinh(ASINH_TOP)
ASINH_SCALE = 32767.0 / ASINH_TOP
GAIN = 2.0 / KNEE
LN2 = math.log(2.0)
PLANES = 4
HALVES = 2
SHARES = PLANES * HALVES
SHEET = DEVS // SHARES


def signed(level, like):
    return jnp.where(like < 0.0, -level, level)


def to_float(code):
    return code.astype(jnp.int32).astype(jnp.float32)


def encode_value(x):
    y = jnp.abs(x) * (1.0 / KNEE)
    level = jnp.log(y + jnp.sqrt(y * y + 1.0)) * ASINH_SCALE + 0.5
    return signed(jnp.minimum(level, 32767.0).astype(jnp.int32), x).astype(jnp.int16)


def decode_value(code):
    angle = to_float(code) * (1.0 / (ASINH_SCALE * LN2))
    return jnp.exp2(angle) - jnp.exp2(-angle)


def power_of(most):
    return jnp.ceil(jnp.log(jnp.maximum(most, 1e-30)) * (8.0 / LN2) + 0.01)


def levels(x, power):
    scaled = x * (jnp.exp(power * (-LN2 / 8.0)) * 32767.0**2)
    root = scaled * lax.rsqrt(jnp.abs(scaled) + 1e-30)
    return jnp.round(root).astype(jnp.int32)


def unit_of(power):
    return jnp.exp(power * (LN2 / 8.0)) * (1.0 / 32767.0**2)


def dot32(a, b, dims=((1,), (0,))):
    return lax.dot_general(a, b, (dims, ((), ())), preferred_element_type=jnp.float32)


def split(x):
    high = x.astype(jnp.bfloat16)
    return high, (x - high.astype(jnp.float32)).astype(jnp.bfloat16)


def encode_kernel(place_ref, e_ref, out_ref):
    for d in range(COLS):
        x = e_ref[:, d * SUB : (d + 1) * SUB]
        tall = jnp.concatenate([x[:, t * 128 : (t + 1) * 128] for t in range(TILES)], axis=0)
        out_ref[0, d] = encode_value(tall)


def encode(eigvecs, place):
    size = COLS * SUB

    def source(k, h, a, place_ref):
        z = lax.rem(place_ref[0] + k, PLANES)
        return 0, (a * PLANES + z) * HALVES + lax.rem(place_ref[1] + h, HALVES)

    return pl.pallas_call(
        encode_kernel,
        out_shape=jax.ShapeDtypeStruct((SHARES, SHEET, OWN * TILES, 128), jnp.int16),
        grid_spec=pltpu.PrefetchScalarGridSpec(
            num_scalar_prefetch=1,
            grid=(PLANES, HALVES, SHEET // COLS),
            in_specs=[pl.BlockSpec((OWN, size), source)],
            out_specs=pl.BlockSpec((1, COLS, OWN * TILES, 128), lambda k, h, a, place_ref: (k * HALVES + h, a, 0, 0)),
        ),
        compiler_params=pltpu.CompilerParams(vmem_limit_bytes=ROOM),
        name="encode",
    )(place, eigvecs)


def gram_kernel(s_ref, slot_ref, *refs):
    arrived, (gram_ref, out_ref, t_ref, refl_ref, held, sems) = refs[:COLS], refs[COLS:]
    for k in range(COLS):
        held[k] = arrived[k][0]
    for p in range(PANELS):
        t_ref[p] = held[s_ref[9 + p]]
    copies = []
    gram = jnp.zeros((PANELS * NB, PANELS * NB), jnp.float32)
    for step in range(STEPS):
        row_ids = s_ref[8] + step * STEP + lax.broadcasted_iota(jnp.int32, (STEP, NB), 0)
        base = row_ids - lax.broadcasted_iota(jnp.int32, (STEP, NB), 1)
        rows = slice(step * STEP, (step + 1) * STEP)
        for p in range(PANELS):
            below = base - s_ref[4 + p]
            unit = jnp.where(below == 0, jnp.float32(1.0), jnp.float32(0.0))
            block = jnp.where(below > 0, slot_ref[s_ref[p], rows, :].astype(jnp.float32), unit)
            refl_ref[rows, p * NB : (p + 1) * NB] = block.astype(jnp.bfloat16)
        v = refl_ref[rows, :]
        part = pl.ds(step * STEP, STEP)
        copies.append(pltpu.make_async_copy(refl_ref.at[part], out_ref.at[part], sems.at[step]))
        copies[-1].start()
        gram += dot32(v, v, ((0,), (0,)))
    blocks = [gram[q * NB : (q + 1) * NB, p * NB : (p + 1) * NB] for q, p in PAIRS]
    most = jnp.zeros((1, 1), jnp.float32)
    for block in blocks:
        most = jnp.maximum(most, jnp.max(jnp.abs(block), axis=(0, 1), keepdims=True))
    power = power_of(most)
    rows = [levels(block, power).astype(jnp.float32) for block in blocks]
    rows += [jnp.zeros((NB, NB), jnp.float32), jnp.broadcast_to(power, (NB, NB))]
    gram_ref[...] = jnp.swapaxes(jnp.stack(rows), 0, 1)
    for copy in copies:
        copy.wait()


def call(kernel, outs, ins, scalars=None, scratch=(), hbm_in=(), hbm_out=()):
    spec, raw = pl.BlockSpec(memory_space=pltpu.VMEM), pl.BlockSpec(memory_space=pltpu.HBM)
    kept = [pltpu.with_memory_space_constraint(x, pltpu.HBM if i in hbm_in else pltpu.VMEM) for i, x in enumerate(ins)]
    head = [] if scalars is None else [scalars]
    return pl.pallas_call(
        kernel,
        out_shape=tuple(pltpu.HBM(*out) if i in hbm_out else pltpu.VMEM(*out) for i, out in enumerate(outs)),
        in_specs=[pl.BlockSpec(memory_space=pltpu.SMEM)] * len(head) + [raw if i in hbm_in else spec for i in range(len(ins))],
        out_specs=tuple(raw if i in hbm_out else spec for i in range(len(outs))),
        scratch_shapes=list(scratch),
        compiler_params=pltpu.CompilerParams(vmem_limit_bytes=ROOM),
    )(*head, *kept)


def gram_of(scalars, slots, triangles):
    outs = (
        ((DEVS, 8, NB), jnp.float32),
        ((SUB, PANELS * NB), jnp.bfloat16),
        ((PANELS, NB, NB), jnp.bfloat16),
    )
    scratch = [
        pltpu.VMEM((SUB, PANELS * NB), jnp.bfloat16),
        pltpu.VMEM((COLS, NB, NB), jnp.bfloat16),
        pltpu.SemaphoreType.DMA((STEPS,)),
    ]
    return call(gram_kernel, outs, (slots, *triangles), scalars, scratch, hbm_out=(1,))


def project_kernel(s_ref, code_ref, refl_hbm, gram_ref, pack_ref, high_ref, low_ref, refl_ref, sem):
    fetch = pltpu.make_async_copy(refl_hbm, refl_ref, sem.at[0])
    fetch.start()
    upper = lax.broadcasted_iota(jnp.int32, (COLS // 2, 8, 128), 1) < OWN
    for r in range(DEVS // COLS):
        a, source, b = r // SHARES, r // HALVES % PLANES, r % HALVES
        share = lax.rem(s_ref[13] + (PLANES - source), PLANES) * HALVES + lax.rem(s_ref[14] + b, HALVES)
        rows = slice(r * COLS * OWN, (r + 1) * COLS * OWN)
        for t in range(0, TILES, 2):
            code = code_ref[a * COLS : (a + 1) * COLS, share, t * OWN : (t + 2) * OWN, :]
            x = decode_value(code).reshape(COLS // 2, 2, 8, 128)
            even, odd = x[:, 0], x[:, 1]
            first = jnp.where(upper, even, pltpu.roll(odd, OWN, 1))
            second = jnp.where(upper, pltpu.roll(even, OWN, 1), odd)
            for k, tile in ((t, first), (t + 1, second)):
                high, low = split(tile.reshape(COLS * OWN, 128))
                high_ref[rows, k * 128 : (k + 1) * 128] = high
                low_ref[rows, k * 128 : (k + 1) * 128] = low
    fetch.wait()
    v = refl_ref[...]
    part = dot32(high_ref[...], v) + dot32(low_ref[...], v)
    each = K // 16
    row = lax.broadcasted_iota(jnp.int32, (each, 8, NB), 1)
    for p in range(PANELS):
        block = part[:, p * NB : (p + 1) * NB].reshape(each, 16, NB)
        power = power_of(jnp.max(jnp.abs(block), axis=(1, 2), keepdims=True))
        where = slice(p * each, (p + 1) * each)
        pack_ref[where, 0:16, :] = levels(block, power).astype(jnp.int16)
        tail = jnp.where(row == 6, power, gram_ref[where])
        pack_ref[where, 16:24, :] = tail.astype(jnp.int32).astype(jnp.int16)


def project(scalars, codes, refl, gram):
    outs = (((DEVS, PACK, NB), jnp.int16),) + (((K, SUB), jnp.bfloat16),) * 2
    scratch = [pltpu.VMEM((SUB, PANELS * NB), jnp.bfloat16), pltpu.SemaphoreType.DMA((1,))]
    return call(project_kernel, outs, (codes, refl, gram), scalars, scratch, hbm_in=(1,))


def total_kernel(in_ref, out_ref):
    level = to_float(in_ref[...])
    value = level * jnp.abs(level)
    proj = jnp.sum(value[:, 0:16] * unit_of(level[:, 22:23]), axis=0)
    gram = jnp.sum(value[:, 16:24] * unit_of(level[:, 23:24]), axis=0)
    row = lax.broadcasted_iota(jnp.int32, (8, NB), 0)
    gram = jnp.where(row < 6, gram, 0.0)
    proj_power = power_of(jnp.max(jnp.abs(proj), axis=(0, 1), keepdims=True))
    gram_power = power_of(jnp.max(jnp.abs(gram), axis=(0, 1), keepdims=True))
    tail = jnp.where(row == 6, proj_power, jnp.where(row == 7, gram_power, levels(gram, gram_power).astype(jnp.float32)))
    code = jnp.concatenate([levels(proj, proj_power), tail.astype(jnp.int32)], axis=0)
    out_ref[...] = jnp.broadcast_to(code[None], out_ref.shape).astype(jnp.int16)


def total(parts):
    return call(total_kernel, (((DEVS // HALVES, PACK, NB), parts.dtype),), (parts,))[0]


def update_kernel(s_ref, mine_ref, other_ref, t_ref, high_ref, low_ref, refl_ref, out_ref, c_high, c_low):
    mine, other = to_float(mine_ref[...]), to_float(other_ref[...])
    first = s_ref[14] == 0
    halves = (jnp.where(first, mine, other), jnp.where(first, other, mine))
    shape = (DEVS // COLS // HALVES, COLS, PACK, NB)
    level = jnp.stack([half.reshape(shape) for half in halves], axis=1).reshape(DEVS, PACK, NB)
    value = level * jnp.abs(level)
    proj = value[:, 0:16] * unit_of(level[:, 22:23])
    blocks = jnp.swapaxes(value[:, 16:24] * unit_of(level[:, 23:24]), 0, 1)
    gram = {pair: split(blocks[b]) for b, pair in enumerate(PAIRS)}
    found = {}
    for p in reversed(range(PANELS)):
        rest = proj[p * 32 : (p + 1) * 32].reshape(K, NB)
        for q in range(p + 1, PANELS):
            (c1, c2), (g1, g2) = found[q], gram[(q, p)]
            rest -= dot32(c1, g1) + (dot32(c1, g2) + dot32(c2, g1))
        triangle = t_ref[p]
        r1, r2 = split(rest)
        dims = ((1,), (1,))
        found[p] = split(dot32(r1, triangle, dims) + dot32(r2, triangle, dims))
        c_high[:, p * NB : (p + 1) * NB] = found[p][0]
        c_low[:, p * NB : (p + 1) * NB] = found[p][1]
    for step in range(STEPS):
        cols = slice(step * STEP, (step + 1) * STEP)
        v = refl_ref[cols, :]
        change = dot32(c_high[...], v, ((1,), (1,))) + dot32(c_low[...], v, ((1,), (1,)))
        back = high_ref[:, cols].astype(jnp.float32) + (low_ref[:, cols].astype(jnp.float32) - change)
        for c in range(COLS):
            block = back[c * WIDE : (c + 1) * WIDE]
            power = power_of(jnp.max(jnp.abs(block), axis=(0, 1), keepdims=True))
            code = levels(block, power).astype(jnp.int16)
            for t in range(STEP // 128):
                at = (step * (STEP // 128) + t) * WIDE
                out_ref[c, at : at + WIDE, :] = code[:, t * 128 : (t + 1) * 128]
            at = TILES * WIDE + step * 8
            out_ref[c, at : at + 8, :] = jnp.broadcast_to(power, (8, 128)).astype(jnp.int32).astype(jnp.int16)


def update(scalars, mine, other, triangles, high, low, refl):
    outs = (((COLS, TILES * WIDE + 8 * STEPS, 128), jnp.int16),)
    scratch = [pltpu.VMEM((K, PANELS * NB), jnp.bfloat16)] * 2
    return call(update_kernel, outs, (mine, other, triangles, high, low, refl), scalars, scratch)[0]


def finish_kernel(code_ref, out_ref, rows, sems):
    copies = []
    for c in range(COLS):
        for k in range(STEPS):
            at = TILES * WIDE + 8 * k
            unit = unit_of(to_float(code_ref[c, at : at + 8, :])) * (1.0 / GAIN)
            unit = jnp.concatenate([unit] * (WIDE // 8), axis=0)
            for t in range(k * (STEP // 128), (k + 1) * (STEP // 128)):
                level = to_float(code_ref[c, t * WIDE : (t + 1) * WIDE, :])
                rows[:, c * SUB + t * 128 : c * SUB + (t + 1) * 128] = level * jnp.abs(level) * unit
        part = (slice(None), pl.ds(c * SUB, SUB))
        copies.append(pltpu.make_async_copy(rows.at[part], out_ref.at[part], sems.at[c]))
        copies[-1].start()
    for copy in copies:
        copy.wait()


def finish(codes):
    return pl.pallas_call(
        finish_kernel,
        out_shape=jax.ShapeDtypeStruct((WIDE, COLS * SUB), jnp.float32),
        in_specs=[pl.BlockSpec(memory_space=pltpu.VMEM)],
        out_specs=pl.BlockSpec(memory_space=pl.ANY),
        scratch_shapes=[pltpu.VMEM((WIDE, COLS * SUB), jnp.float32), pltpu.SemaphoreType.DMA((COLS,))],
        compiler_params=pltpu.CompilerParams(vmem_limit_bytes=ROOM),
        name="finish",
    )(pltpu.with_memory_space_constraint(codes, pltpu.VMEM))


def exchange(x, axis):
    return lax.all_to_all(x, axis, split_axis=0, concat_axis=0, tiled=True)


def spread(x):
    blocks = [x]
    for k in range(1, COLS):
        blocks.append(lax.ppermute(x, "col", [(c, c ^ k) for c in range(COLS)]))
    return blocks


def across(sent):
    shares = [sent[0]]
    for share in range(1, SHARES):
        k, h = share // HALVES, share % HALVES
        pairs = []
        for r in range(DEVS // COLS):
            z, core = r // HALVES % PLANES, r % HALVES
            pairs.append((r, r + ((z + k) % PLANES - z) * HALVES + (core + h) % HALVES - core))
        shares.append(lax.ppermute(sent[share], "row", pairs))
    packed = jnp.concatenate(shares, axis=1)
    return packed.reshape(SHEET, SHARES, OWN * TILES, 128)


def within(x, size):
    groups = []
    for share in range(size):
        rows = [r for r in range(DEVS // COLS) if r % size == share]
        groups.append([r * COLS + c for r in rows for c in range(COLS)])
    return lax.all_to_all(x, ALL, split_axis=0, concat_axis=0, tiled=True, axis_index_groups=groups)


def local(eigvecs, panels, tfactors, owners, offsets):
    row, col = lax.axis_index("row"), lax.axis_index("col")
    place = jnp.stack([row // HALVES % PLANES, row % HALVES])
    own = jnp.stack([(row * COLS + col) * SUB])
    scalars = jnp.concatenate([owners, offsets, own, owners ^ col, place])
    slots = exchange(panels.reshape(COLS, SUB, NB), "col")
    triangles = spread(tfactors)
    planes = encode(eigvecs, place)
    sent, slots = lax.optimization_barrier((across(planes), slots))
    codes = within(sent, SHARES)
    gram, refl, triangles = gram_of(scalars, slots, triangles)
    pack, high, low = project(scalars, codes, refl, gram)
    mine = within(total(exchange(pack, ALL)), HALVES)
    other = lax.ppermute(mine, "row", [(r, r ^ 1) for r in range(DEVS // COLS)])
    out = update(scalars, mine, other, triangles, high, low, refl)
    return finish(exchange(out, "col"))


def solution(mesh):
    in_specs = (P(ALL, None), P("col", "row", None), P("col", None, None), P(), P())
    out_specs = P("col", "row")
    return jax.shard_map(local, mesh=mesh, in_specs=in_specs, out_specs=out_specs, check_vma=False)
```

```python
import math

import jax
import jax.numpy as jnp
from jax import lax
from jax.experimental import pallas as pl
from jax.experimental.pallas import tpu as pltpu
from jax.sharding import PartitionSpec as P


PANELS = 4
NB = 128
K = 512
DEVS = 128
COLS = 8
OWN = 4
SUB = 2048
STEP = 512
STEPS = SUB // STEP
TILES = SUB // 128
HALVES = 2
PLANES = 4
PEERS = DEVS // HALVES
MINE = K // HALVES
BOTH = SUB * HALVES
WIDE = MINE // COLS
SPAN = 1024
SPANS = SUB // SPAN
PACK = 32
PAIRS = [(q, p) for q in range(PANELS) for p in range(q)]
ALL = ("row", "col")
ROOM = 24 << 20

ASINH_TOP = 12.5
KNEE = 6.0 / math.sinh(ASINH_TOP)
ASINH_SCALE = 32767.0 / ASINH_TOP
GAIN = 2.0 / KNEE
LN2 = math.log(2.0)
SHARES = PLANES * HALVES
SHEET = DEVS // SHARES


def signed(level, like):
    return jnp.where(like < 0.0, -level, level)


def to_float(code):
    return code.astype(jnp.int32).astype(jnp.float32)


def encode_value(x):
    y = jnp.abs(x) * (1.0 / KNEE)
    level = jnp.log(y + jnp.sqrt(y * y + 1.0)) * ASINH_SCALE + 0.5
    return signed(jnp.minimum(level, 32767.0).astype(jnp.int32), x).astype(jnp.int16)


def decode_value(code):
    angle = to_float(code) * (1.0 / (ASINH_SCALE * LN2))
    return jnp.exp2(angle) - jnp.exp2(-angle)


def power_of(most):
    return jnp.ceil(jnp.log(jnp.maximum(most, 1e-30)) * (8.0 / LN2) + 0.01)


def levels(x, power):
    scaled = x * (jnp.exp(power * (-LN2 / 8.0)) * 32767.0**2)
    root = scaled * lax.rsqrt(jnp.abs(scaled) + 1e-30)
    return jnp.round(root).astype(jnp.int32)


def unit_of(power):
    return jnp.exp(power * (LN2 / 8.0)) * (1.0 / 32767.0**2)


def dot32(a, b, dims=((1,), (0,))):
    return lax.dot_general(a, b, (dims, ((), ())), preferred_element_type=jnp.float32)


def split(x):
    high = x.astype(jnp.bfloat16)
    return high, (x - high.astype(jnp.float32)).astype(jnp.bfloat16)


def encode_kernel(place_ref, e_ref, out_ref):
    for d in range(COLS):
        x = e_ref[:, d * SUB : (d + 1) * SUB]
        tall = jnp.concatenate([x[:, t * 128 : (t + 1) * 128] for t in range(TILES)], axis=0)
        out_ref[0, d, 0] = encode_value(tall)


def encode(eigvecs, place):
    size = COLS * SUB

    def source(k, a, h, place_ref):
        return 0, (a * PLANES + lax.rem(place_ref[0] + k, PLANES)) * HALVES + h

    return pl.pallas_call(
        encode_kernel,
        out_shape=jax.ShapeDtypeStruct((PLANES, SHEET, HALVES, OWN * TILES, 128), jnp.int16),
        grid_spec=pltpu.PrefetchScalarGridSpec(
            num_scalar_prefetch=1,
            grid=(PLANES, SHEET // COLS, HALVES),
            in_specs=[pl.BlockSpec((OWN, size), source)],
            out_specs=pl.BlockSpec((1, COLS, 1, OWN * TILES, 128), lambda k, a, h, place_ref: (k, a, h, 0, 0)),
        ),
        compiler_params=pltpu.CompilerParams(vmem_limit_bytes=ROOM),
        name="encode",
    )(place, eigvecs)


def mask_kernel(s_ref, slot_ref, out_ref, refl_ref, sems):
    copies = []
    for step in range(STEPS):
        row_ids = s_ref[8] + step * STEP + lax.broadcasted_iota(jnp.int32, (STEP, NB), 0)
        base = row_ids - lax.broadcasted_iota(jnp.int32, (STEP, NB), 1)
        rows = slice(step * STEP, (step + 1) * STEP)
        for p in range(PANELS):
            below = base - s_ref[4 + p]
            unit = jnp.where(below == 0, jnp.float32(1.0), jnp.float32(0.0))
            block = jnp.where(below > 0, slot_ref[s_ref[p], rows, :].astype(jnp.float32), unit)
            refl_ref[rows, p * NB : (p + 1) * NB] = block.astype(jnp.bfloat16)
        part = pl.ds(step * STEP, STEP)
        copies.append(pltpu.make_async_copy(refl_ref.at[part], out_ref.at[part], sems.at[step]))
        copies[-1].start()
    for copy in copies:
        copy.wait()


def fetch_both(refl_hbm, other_hbm, refl_ref, sems):
    fetches = []
    for h, source in enumerate((refl_hbm, other_hbm)):
        fetches.append(pltpu.make_async_copy(source, refl_ref.at[pl.ds(h * SUB, SUB)], sems.at[h]))
        fetches[-1].start()
    return fetches


def gram_kernel(s_ref, refl_hbm, other_hbm, *refs):
    arrived, (gram_ref, t_ref, held, refl_ref, sems) = refs[:COLS], refs[COLS:]
    fetches = fetch_both(refl_hbm, other_hbm, refl_ref, sems)
    for k in range(COLS):
        held[k] = arrived[k][0]
    for p in range(PANELS):
        t_ref[p] = held[s_ref[9 + p]]
    for fetch in fetches:
        fetch.wait()
    v = refl_ref[...]
    gram = dot32(v, v, ((0,), (0,)))
    blocks = [gram[q * NB : (q + 1) * NB, p * NB : (p + 1) * NB] for q, p in PAIRS]
    most = jnp.zeros((1, 1), jnp.float32)
    for block in blocks:
        most = jnp.maximum(most, jnp.max(jnp.abs(block), axis=(0, 1), keepdims=True))
    power = power_of(most)
    rows = []
    for block in blocks:
        level = levels(block, power).astype(jnp.float32)
        rows += [level[0:PEERS], level[PEERS:NB]]
    rows += [jnp.zeros((PEERS, NB), jnp.float32)] * 3 + [jnp.broadcast_to(power, (PEERS, NB))]
    gram_ref[...] = jnp.swapaxes(jnp.stack(rows), 0, 1)


def call(kernel, outs, ins, scalars=None, scratch=(), hbm_in=(), hbm_out=()):
    spec, raw = pl.BlockSpec(memory_space=pltpu.VMEM), pl.BlockSpec(memory_space=pltpu.HBM)
    kept = [pltpu.with_memory_space_constraint(x, pltpu.HBM if i in hbm_in else pltpu.VMEM) for i, x in enumerate(ins)]
    head = [] if scalars is None else [scalars]
    return pl.pallas_call(
        kernel,
        out_shape=tuple(pltpu.HBM(*out) if i in hbm_out else pltpu.VMEM(*out) for i, out in enumerate(outs)),
        in_specs=[pl.BlockSpec(memory_space=pltpu.SMEM)] * len(head) + [raw if i in hbm_in else spec for i in range(len(ins))],
        out_specs=tuple(raw if i in hbm_out else spec for i in range(len(outs))),
        scratch_shapes=list(scratch),
        compiler_params=pltpu.CompilerParams(vmem_limit_bytes=ROOM),
    )(*head, *kept)


def fetch_room():
    return pltpu.VMEM((BOTH, PANELS * NB), jnp.bfloat16), pltpu.SemaphoreType.DMA((HALVES,))


def mask(scalars, slots):
    outs = (((SUB, PANELS * NB), jnp.bfloat16),)
    scratch = [pltpu.VMEM((SUB, PANELS * NB), jnp.bfloat16), pltpu.SemaphoreType.DMA((STEPS,))]
    return call(mask_kernel, outs, (slots,), scalars, scratch, hbm_out=(0,))[0]


def gram_of(scalars, refl, other, triangles):
    outs = (((PEERS, 16, NB), jnp.float32), ((PANELS, NB, NB), jnp.bfloat16))
    scratch = [pltpu.VMEM((COLS, NB, NB), jnp.bfloat16), *fetch_room()]
    return call(gram_kernel, outs, (refl, other, *triangles), scalars, scratch, hbm_in=(0, 1))


def project_kernel(s_ref, code_ref, refl_hbm, other_hbm, gram_ref, pack_ref, high_ref, low_ref, refl_ref, sems):
    fetches = fetch_both(refl_hbm, other_hbm, refl_ref, sems)
    upper = lax.broadcasted_iota(jnp.int32, (COLS // 2, 8, 128), 1) < OWN
    for r in range(PEERS // COLS):
        a, source = r // PLANES, r % PLANES
        turn = lax.rem(s_ref[13] + (PLANES - source), PLANES) * HALVES
        rows = slice(r * COLS * OWN, (r + 1) * COLS * OWN)
        for h in range(HALVES):
            share = turn + lax.rem(s_ref[14] + h, HALVES)
            for t in range(0, TILES, 2):
                code = code_ref[a * COLS : (a + 1) * COLS, share, t * OWN : (t + 2) * OWN, :]
                x = decode_value(code).reshape(COLS // 2, 2, 8, 128)
                even, odd = x[:, 0], x[:, 1]
                first = jnp.where(upper, even, pltpu.roll(odd, OWN, 1))
                second = jnp.where(upper, pltpu.roll(even, OWN, 1), odd)
                for k, tile in ((h * TILES + t, first), (h * TILES + t + 1, second)):
                    high, low = split(tile.reshape(COLS * OWN, 128))
                    high_ref[rows, k * 128 : (k + 1) * 128] = high
                    low_ref[rows, k * 128 : (k + 1) * 128] = low
    for fetch in fetches:
        fetch.wait()
    v = refl_ref[...]
    part = dot32(high_ref[...], v) + dot32(low_ref[...], v)
    each = MINE // 16
    row = lax.broadcasted_iota(jnp.int32, (each, 16, NB), 1)
    for p in range(PANELS):
        block = part[:, p * NB : (p + 1) * NB].reshape(each, 16, NB)
        power = power_of(jnp.max(jnp.abs(block), axis=(1, 2), keepdims=True))
        where = slice(p * each, (p + 1) * each)
        pack_ref[where, 0:16, :] = levels(block, power).astype(jnp.int16)
        tail = jnp.where(row == 14, power, gram_ref[where])
        pack_ref[where, 16:32, :] = tail.astype(jnp.int32).astype(jnp.int16)


def project(scalars, codes, refl, other, gram):
    outs = (((PEERS, PACK, NB), jnp.int16),) + (((MINE, BOTH), jnp.bfloat16),) * 2
    return call(project_kernel, outs, (codes, refl, other, gram), scalars, fetch_room(), hbm_in=(1, 2))


def total_kernel(in_ref, out_ref):
    level = to_float(in_ref[...])
    value = level * jnp.abs(level)
    proj = jnp.sum(value[:, 0:16] * unit_of(level[:, 30:31]), axis=0)
    gram = jnp.sum(value[:, 16:32] * unit_of(level[:, 31:32]), axis=0)
    row = lax.broadcasted_iota(jnp.int32, (16, NB), 0)
    gram = jnp.where(row < 12, gram, 0.0)
    proj_power = power_of(jnp.max(jnp.abs(proj), axis=(0, 1), keepdims=True))
    gram_power = power_of(jnp.max(jnp.abs(gram), axis=(0, 1), keepdims=True))
    tail = levels(gram, gram_power).astype(jnp.float32)
    tail = jnp.where(row == 14, proj_power, jnp.where(row == 15, gram_power, tail))
    code = jnp.concatenate([levels(proj, proj_power), tail.astype(jnp.int32)], axis=0)
    out_ref[...] = jnp.broadcast_to(code[None], out_ref.shape).astype(jnp.int16)


def total(parts):
    return call(total_kernel, ((parts.shape, parts.dtype),), (parts,))[0]


def update_kernel(s_ref, sums_ref, t_ref, high_ref, low_ref, refl_ref, other_ref, out_ref, c_high, c_low):
    level = to_float(sums_ref[...])
    value = level * jnp.abs(level)
    proj = value[:, 0:16] * unit_of(level[:, 30:31])
    halves = jnp.swapaxes(value[:, 16:32] * unit_of(level[:, 31:32]), 0, 1)
    gram = {}
    for b, pair in enumerate(PAIRS):
        gram[pair] = split(jnp.concatenate([halves[2 * b], halves[2 * b + 1]], axis=0))
    found = {}
    for p in reversed(range(PANELS)):
        rest = proj[p * 16 : (p + 1) * 16].reshape(MINE, NB)
        for q in range(p + 1, PANELS):
            (c1, c2), (g1, g2) = found[q], gram[(q, p)]
            rest -= dot32(c1, g1) + (dot32(c1, g2) + dot32(c2, g1))
        triangle = t_ref[p]
        r1, r2 = split(rest)
        dims = ((1,), (1,))
        found[p] = split(dot32(r1, triangle, dims) + dot32(r2, triangle, dims))
        c_high[:, p * NB : (p + 1) * NB] = found[p][0]
        c_low[:, p * NB : (p + 1) * NB] = found[p][1]
    for step in range(HALVES * SPANS):
        h, k = step // SPANS, step % SPANS
        cols = slice(step * SPAN, (step + 1) * SPAN)
        v = (refl_ref, other_ref)[h][k * SPAN : (k + 1) * SPAN, :]
        change = dot32(c_high[...], v, ((1,), (1,))) + dot32(c_low[...], v, ((1,), (1,)))
        back = high_ref[:, cols].astype(jnp.float32) + (low_ref[:, cols].astype(jnp.float32) - change)
        to = lax.rem(s_ref[14] + h, HALVES) * COLS
        for c in range(COLS):
            block = back[c * WIDE : (c + 1) * WIDE]
            power = power_of(jnp.max(jnp.abs(block), axis=(0, 1), keepdims=True))
            code = levels(block, power).astype(jnp.int16)
            for t in range(SPAN // 128):
                at = (k * (SPAN // 128) + t) * WIDE
                out_ref[to + c, at : at + WIDE, :] = code[:, t * 128 : (t + 1) * 128]
            at = TILES * WIDE + k * 8
            out_ref[to + c, at : at + 8, :] = jnp.broadcast_to(power, (8, 128)).astype(jnp.int32).astype(jnp.int16)


def update(scalars, sums, triangles, high, low, refl, other):
    outs = (((HALVES * COLS, TILES * WIDE + 8 * SPANS, 128), jnp.int16),)
    scratch = [pltpu.VMEM((MINE, PANELS * NB), jnp.bfloat16)] * 2
    return call(update_kernel, outs, (sums, triangles, high, low, refl, other), scalars, scratch)[0]


def finish_kernel(code_ref, out_ref, rows, sems):
    copies = []
    for c in range(COLS):
        for h in range(HALVES):
            lines = slice(h * WIDE, (h + 1) * WIDE)
            for k in range(SPANS):
                at = TILES * WIDE + 8 * k
                unit = unit_of(to_float(code_ref[h * COLS + c, at : at + 8, :])) * (1.0 / GAIN)
                unit = jnp.concatenate([unit] * (WIDE // 8), axis=0)
                for t in range(k * (SPAN // 128), (k + 1) * (SPAN // 128)):
                    level = to_float(code_ref[h * COLS + c, t * WIDE : (t + 1) * WIDE, :])
                    rows[lines, c * SUB + t * 128 : c * SUB + (t + 1) * 128] = level * jnp.abs(level) * unit
        part = (slice(None), pl.ds(c * SUB, SUB))
        copies.append(pltpu.make_async_copy(rows.at[part], out_ref.at[part], sems.at[c]))
        copies[-1].start()
    for copy in copies:
        copy.wait()


def finish(codes):
    return pl.pallas_call(
        finish_kernel,
        out_shape=jax.ShapeDtypeStruct((K // COLS, COLS * SUB), jnp.float32),
        in_specs=[pl.BlockSpec(memory_space=pltpu.VMEM)],
        out_specs=pl.BlockSpec(memory_space=pl.ANY),
        scratch_shapes=[pltpu.VMEM((K // COLS, COLS * SUB), jnp.float32), pltpu.SemaphoreType.DMA((COLS,))],
        compiler_params=pltpu.CompilerParams(vmem_limit_bytes=ROOM),
        name="finish",
    )(pltpu.with_memory_space_constraint(codes, pltpu.VMEM))


def exchange(x, axis):
    return lax.all_to_all(x, axis, split_axis=0, concat_axis=0, tiled=True)


def spread(x):
    blocks = [x]
    for k in range(1, COLS):
        blocks.append(lax.ppermute(x, "col", [(c, c ^ k) for c in range(COLS)]))
    return blocks


def across(sent):
    sent = sent.reshape(PLANES, SHEET, HALVES * OWN * TILES, 128)
    shares = [sent[0]]
    for k in range(1, PLANES):
        pairs = []
        for r in range(DEVS // COLS):
            z = r // HALVES % PLANES
            pairs.append((r, r + ((z + k) % PLANES - z) * HALVES))
        shares.append(lax.ppermute(sent[k], "row", pairs))
    packed = jnp.concatenate(shares, axis=1)
    return packed.reshape(SHEET, SHARES, OWN * TILES, 128)


def to_owners(x):
    groups = [[(r + h) * COLS + c for h in range(HALVES) for c in range(COLS)] for r in range(0, DEVS // COLS, HALVES)]
    return lax.all_to_all(x, ALL, split_axis=0, concat_axis=0, tiled=True, axis_index_groups=groups)


def within(x, size):
    groups = []
    for share in range(size):
        rows = [r for r in range(DEVS // COLS) if r % size == share]
        groups.append([r * COLS + c for r in rows for c in range(COLS)])
    return lax.all_to_all(x, ALL, split_axis=0, concat_axis=0, tiled=True, axis_index_groups=groups)


def local(eigvecs, panels, tfactors, owners, offsets):
    row, col = lax.axis_index("row"), lax.axis_index("col")
    place = jnp.stack([row // HALVES % PLANES, row % HALVES])
    own = jnp.stack([(row * COLS + col) * SUB])
    scalars = jnp.concatenate([owners, offsets, own, owners ^ col, place])
    slots = exchange(panels.reshape(COLS, SUB, NB), "col")
    triangles = spread(tfactors)
    planes = encode(eigvecs, place)
    sent, slots = lax.optimization_barrier((across(planes), slots))
    codes = within(sent, SHARES)
    refl = mask(scalars, slots)
    other = lax.ppermute(refl, "row", [(r, r ^ 1) for r in range(DEVS // COLS)])
    gram, triangles = gram_of(scalars, refl, other, triangles)
    pack, high, low = project(scalars, codes, refl, other, gram)
    sums = within(total(within(pack, HALVES)), HALVES)
    out = update(scalars, sums, triangles, high, low, refl, other)
    return finish(to_owners(out))


def solution(mesh):
    in_specs = (P(ALL, None), P("col", "row", None), P("col", None, None), P(), P())
    out_specs = P("col", "row")
    return jax.shard_map(local, mesh=mesh, in_specs=in_specs, out_specs=out_specs, check_vma=False)
```
